32 devices in a mesh: groups: 2 (over y), space: 16 (over z, x, core).
Axes of the slice: x: 2, y: 2, z: 4, core: 2. Of those that a mesh axis runs over, the one named last changes fastest.
Arguments:
- modes: float32 [4, 128, 32, 64], P('groups', None, 'space'), parts along dimension 0, may hold values from -6 to 6
- cell_weight: float32 [32, 128], P('space', 'groups'), parts along dimension 1, may hold values from 0.5 to 2
- seeds: int32 [256], P(('groups', 'space')), parts along dimension 0, may hold values from 0 to 255
- coeff_table: float32 [256, 128], replicated, may hold values from -6 to 6
- force_table: float32 [256, 128], replicated, may hold values from -6 to 6
- visc_table: float32 [256], replicated, may hold values from 0.02 to 0.2
Outputs:
- coefficients: float32 [256, 128], P(('groups', 'space')), parts along dimension 0
The draws below stay inside these ranges and needn't reach their ends.
There are 2 independent parts, one for each index of `groups`. The reference program is written for one: setup_inputs(seed, part) draws one part's arguments, and reference() takes and returns one part's arrays. A program takes and returns all parts, laid end to end along the dimension named above; an argument that names none is the same for every part. Nothing has to cross between parts.
All inputs are finite; a program needn't handle non-finite values.
Results may differ from the reference program's by a relative error of at most 0.00013.
Values sent between devices are 32-bit elements; how exact they have to be, the bound alone decides.
A program may use at most 64 MiB of HBM per device.

```python
import math
import jax
import jax.numpy as jnp
from jax import lax

M = 128
NY = 64
PARAMS = 256
STEPS = 2
NX = 32
TRAJ = 128


def plant(drawn, rng, low, top_value):
    longest = drawn.shape.index(max(drawn.shape))
    spots = []
    for shift in (0, 1):
        where = [jax.random.randint(jax.random.fold_in(rng, axis), (), 0, length) for axis, length in enumerate(drawn.shape)]
        where[longest] = (where[longest] + shift) % drawn.shape[longest]
        spots.append(tuple(where))
    return drawn.at[spots[0]].set(low).at[spots[1]].set(top_value)


def block_scale(stream_key, extent, shards, smallest, top_value):
    factor_of = 1.0
    for axis_at, parts in shards:
        steps = jax.random.uniform(jax.random.fold_in(jax.random.fold_in(stream_key, 6), axis_at), (parts,), jnp.float32, smallest / len(shards), top_value / len(shards))
        factor_of = factor_of * jnp.repeat(jnp.exp(steps), extent[axis_at] // parts).reshape((-1,) + (1,) * (len(extent) - 1 - axis_at))
    return factor_of


def scatter_about(stream_key, extent, deviation, reach, shards=(), held_as=jnp.bfloat16):
    values = deviation * jax.random.normal(stream_key, extent, jnp.float32)
    if shards:
        values = values * block_scale(stream_key, extent, shards, -0.22, 0.18)
    return jnp.clip(values, -reach, reach).astype(held_as)


def setup_inputs(seed: int = 0, part: int = 0) -> dict:
    streams_of = jax.random.split(jax.random.key(seed), 7)
    part_keys = jax.random.split(jax.random.fold_in(streams_of[6], part), 7)
    return {
        "modes": scatter_about(part_keys[0], (2, M, NX, NY), 1.0, 6.0, ((2, 16),), jnp.float32),
        "cell_weight": jnp.clip(jnp.exp(math.log(2.0) - 1.3862944 * jax.random.uniform(part_keys[1], (NX, NY), jnp.float32) ** block_scale(part_keys[1], (NX, NY), ((0, 16),), -0.2, 0.2)), 0.5, 2.0),
        "seeds": plant(jax.random.randint(part_keys[2], (TRAJ,), 0, PARAMS), jax.random.fold_in(part_keys[2], 1), 0, PARAMS - 1).astype(jnp.int32),
        "coeff_table": scatter_about(streams_of[3], (PARAMS, M), 1.0, 6.0, (), jnp.float32),
        "force_table": scatter_about(streams_of[4], (PARAMS, M), 1.0, 6.0, (), jnp.float32),
        "visc_table": jnp.clip(jnp.exp(jax.random.uniform(streams_of[5], (PARAMS,), jnp.float32, math.log(0.02), math.log(0.2))), 0.02, 0.2),
    }


TIME_STEP = 0.5


def slopes_of(modes):
    along = (jnp.roll(modes, 2, 2) - 8.0 * jnp.roll(modes, 1, 2) + 8.0 * jnp.roll(modes, -1, 2) - jnp.roll(modes, -2, 2)) / 12.0
    across = (jnp.roll(modes, 2, 3) - 8.0 * jnp.roll(modes, 1, 3) + 8.0 * jnp.roll(modes, -1, 3) - jnp.roll(modes, -2, 3)) / 12.0
    return jnp.stack([along, across])


def reference(modes, cell_weight, seeds, coeff_table, force_table, visc_table):
    cell_count = NX * NY
    slopes = slopes_of(modes).reshape(2, 2, M, cell_count)
    velocity = modes.reshape(2, M, cell_count)
    cell_scale = cell_weight.reshape(cell_count) / cell_count
    weighted = velocity * cell_scale[None, None, :]
    diffusion = jnp.einsum("taic,tajc->ij", slopes * cell_scale[None, None, None, :], slopes, precision=lax.Precision.HIGHEST)
    block_size = 4

    def project(block_index):
        weighted_block = lax.dynamic_slice_in_dim(weighted, block_index * block_size, block_size, 1)
        advected = jnp.sum(weighted_block[None, :, :, None, :] * slopes[:, :, None, :, :], axis=1)
        return jnp.einsum("tjc,tikc->ijk", velocity, advected, precision=lax.Precision.HIGHEST)

    tensor = lax.map(project, jnp.arange(M // block_size, dtype=jnp.int32)).reshape(M * M, M)
    selector = (seeds[:, None] == jnp.arange(PARAMS, dtype=jnp.int32)[None, :]).astype(jnp.float32)
    coeffs = jnp.dot(selector, coeff_table, precision=lax.Precision.HIGHEST)
    forcing = jnp.dot(selector, force_table, precision=lax.Precision.HIGHEST)
    viscosity = jnp.dot(selector, visc_table, precision=lax.Precision.HIGHEST)
    for repeat in range(STEPS):
        paired = jnp.dot(coeffs, tensor.T, precision=lax.Precision.HIGHEST).reshape(TRAJ, M, M)
        quadratic = jnp.sum(paired * coeffs[:, None, :], axis=2)
        linear = jnp.dot(coeffs, diffusion, precision=lax.Precision.HIGHEST)
        coeffs = coeffs + TIME_STEP * (forcing - viscosity[:, None] * linear - quadratic)
    return coeffs
```

```python
import functools

import jax
import jax.numpy as jnp
from jax import lax
from jax.experimental import pallas as pl
from jax.experimental.pallas import tpu as pltpu
from jax.sharding import PartitionSpec as P

TIME_STEP = 0.5

MESH = pl.DeviceIdType.MESH

ROWS = ((1,), (0,))
LANES = ((1,), (1,))

ROW = 4

TAIL = 8


def product(a, b, contract):
    return lax.dot_general(a, b, (contract, ((), ())), preferred_element_type=jnp.float32)


def split(x, count):
    terms = []
    for _ in range(count):
        terms.append(x.astype(jnp.bfloat16))
        x = x - terms[-1].astype(jnp.float32)
    return terms


def stack(x, count):
    terms = []
    for _ in range(count):
        terms.append(x.astype(jnp.bfloat16).astype(jnp.float32))
        x = x - terms[-1]
    return jnp.concatenate(terms, axis=0).astype(jnp.bfloat16)


def kernel(
    n,
    across,
    modes_hbm,
    weight_hbm,
    seeds_hbm,
    visc_hbm,
    coeff_hbm,
    force_hbm,
    out_ref,
    slabs,
    high,
    mid,
    low,
    speeds,
    weight_ref,
    seeds_ref,
    visc_ref,
    coeff_ref,
    force_ref,
    picks,
    partial,
    landed,
    now_ref,
    push_ref,
    last,
    last_landed,
    load_sem,
    send_sem,
    recv_sem,
    small_sem,
    ok,
):
    me = lax.axis_index("space")
    rows = n // ROW
    row, seat = me // ROW, lax.rem(me, ROW)
    base = me - seat
    side, core = seat // 2, lax.rem(seat, 2)
    own = seeds_hbm.shape[0]
    depth = modes_hbm.shape[0]
    cells = depth // 2
    layers = weight_hbm.shape[0]
    params = coeff_hbm.shape[0]
    total = own * rows
    partner = me + 1 - 2 * core
    mirror = me + 2 - 4 * side
    above = lax.rem(row + 1, rows) * ROW
    below = lax.rem(row + rows - 1, rows) * ROW
    first, final = seat == 0, seat == ROW - 1
    place = seat + 1

    loads = [
        pltpu.make_async_copy(source, target, load_sem.at[i])
        for i, (source, target) in enumerate(
            (
                (modes_hbm, slabs.at[place, pl.ds(0, depth)]),
                (weight_hbm, weight_ref),
                (seeds_hbm, seeds_ref),
                (coeff_hbm, coeff_ref),
                (force_hbm, force_ref),
                (visc_hbm, visc_ref),
            )
        )
    ]
    for load in loads:
        load.start()

    barrier = pltpu.get_barrier_semaphore()

    def tell(peer):
        pl.semaphore_signal(barrier, inc=1, device_id={"space": peer}, device_id_type=MESH)

    def in_column(d):
        return lax.rem(me + ROW * d, n)

    bottom, top = row == 0, row == rows - 1

    @pl.when(core == 0)
    def _():
        tell(partner)

    @pl.when(side == 0)
    def _():
        tell(mirror)

    @pl.when(first & bottom)
    def _():
        tell(below + ROW - 1)
        tell(below + 1)

    @pl.when((seat == 2) & bottom)
    def _():
        tell(below + ROW - 1)

    @pl.when((seat == 1) & jnp.logical_not(top))
    def _():
        tell(above)

    @pl.when(final & jnp.logical_not(top))
    def _():
        tell(above)
        tell(above + 2)

    @pl.loop(row + 1, rows)
    def _(r):
        tell(r * ROW + seat)

    def answer(at, peer):
        pl.semaphore_signal(ok.at[at], inc=1, device_id={"space": peer}, device_id_type=MESH)

    def send(kind, source, target, peer):
        pltpu.make_async_remote_copy(
            src_ref=slabs.at[source],
            dst_ref=slabs.at[target],
            send_sem=send_sem.at[kind],
            recv_sem=recv_sem.at[target],
            device_id={"space": peer},
            device_id_type=MESH,
        ).start()

    def waiting(ref, send_at, recv_at):
        return pltpu.make_async_remote_copy(
            src_ref=ref,
            dst_ref=ref,
            send_sem=send_at,
            recv_sem=recv_at,
            device_id={"space": partner},
            device_id_type=MESH,
        )

    def arrived(slot):
        waiting(slabs.at[slot], send_sem.at[0], recv_sem.at[slot]).wait_recv()

    def spread(phase, source, target):
        @pl.loop(1, rows)
        def _(d):
            pltpu.make_async_remote_copy(
                src_ref=source(lax.rem(row + d, rows)),
                dst_ref=target(d),
                send_sem=send_sem.at[2 + phase],
                recv_sem=small_sem.at[phase],
                device_id={"space": in_column(d)},
                device_id_type=MESH,
            ).start()

    loads[2].wait()
    row_of = lax.broadcasted_iota(jnp.int32, (own, 128), 0)
    picked = jnp.zeros((own, 128), jnp.int32)
    for r in range(own):
        picked = jnp.where(row_of == r, seeds_ref[r], picked)
    picks[row] = picked
    loads[1].wait()
    weight = [weight_ref[s : s + 1, :] for s in range(layers)]
    slabs[place, depth : depth + 1, :] = jnp.concatenate(weight, axis=1) / (cells * n)
    loads[0].wait()

    def seeds_to(r):
        pltpu.make_async_remote_copy(
            src_ref=picks.at[row],
            dst_ref=picks.at[row],
            send_sem=send_sem.at[2],
            recv_sem=small_sem.at[0],
            device_id={"space": r * ROW + seat},
            device_id_type=MESH,
        ).start()

    def outer_down():
        send(1, place, ROW + 1, below + 1)
        send(1, place, ROW + 1, below + ROW - 1)

    def outer_up():
        send(1, place, 0, above)
        send(1, place, 0, above + 2)

    lower = core + side + row
    lower += jnp.where(jnp.logical_not(bottom) & first, 2, 0)
    lower += jnp.where(jnp.logical_not(bottom) & (seat == 2), 1, 0)
    lower += jnp.where(top & final, 2, 0) + jnp.where(top & (seat == 1), 1, 0)
    @pl.when(lower > 0)
    def _():
        pl.semaphore_wait(barrier, lower)

    @pl.when(core == 1)
    def _():
        answer(0, partner)
        send(0, place, place, partner)

    @pl.when(side == 1)
    def _():
        answer(1, mirror)
        send(0, place, place, mirror)

    @pl.when(top & final)
    def _():
        answer(2, above)

    @pl.when(top & (seat == 1))
    def _():
        answer(2, above)

    @pl.when(jnp.logical_not(bottom) & (first | (seat == 2)))
    def _():
        answer(2, below + ROW - 1)

    @pl.loop(0, row)
    def _(r):
        answer(3, r * ROW + seat)
        seeds_to(r)

    @pl.when(first & jnp.logical_not(bottom))
    def _():
        outer_down()

    @pl.when(final & top)
    def _():
        outer_up()

    @pl.when(core == 0)
    def _():
        pl.semaphore_wait(ok.at[0], 1)
        send(0, place, place, partner)

    @pl.when(side == 0)
    def _():
        pl.semaphore_wait(ok.at[1], 1)
        send(0, place, place, mirror)

    @pl.when(final & jnp.logical_not(top))
    def _():
        pl.semaphore_wait(ok.at[2], 2)
        outer_up()

    @pl.when(first & bottom)
    def _():
        pl.semaphore_wait(ok.at[2], 2)
        outer_down()

    @pl.when(jnp.logical_not(top))
    def _():
        pl.semaphore_wait(ok.at[3], rows - 1 - row)

    @pl.loop(row + 1, rows)
    def _(r):
        seeds_to(r)

    def take(slot):
        high[slot], mid[slot], low[slot] = split(slabs[slot, 0:depth, :], 3)

    across_of = seat + 2 - 4 * side + 1
    beside = partner - base + 1
    far = mirror + 1 - 2 * core - base + 1
    take(place)
    arrived(beside)
    take(beside)
    arrived(across_of)
    send(0, across_of, across_of, partner)
    take(across_of)

    for load in loads[3:]:
        load.wait()
    waiting(picks.at[pl.ds(0, rows - 1)], send_sem.at[2], small_sem.at[0]).wait_recv()
    picked = jnp.concatenate([picks[...].reshape(total, 128)] * (params // 128), axis=1)
    chosen = picked == lax.broadcasted_iota(jnp.int32, (total, params), 1)
    viscosity = jnp.sum(jnp.where(chosen, visc_ref[...], 0.0), axis=1, keepdims=True)
    chosen = chosen.astype(jnp.float32)
    coeffs = lax.dot(chosen, coeff_ref[...], precision=lax.Precision.HIGHEST)
    forcing = lax.dot(chosen, force_ref[...], precision=lax.Precision.HIGHEST)

    def speeds_of(now, terms):
        one = product(now, terms[0], LANES)
        two = product(now[: 2 * total], terms[1], LANES)
        three = product(now[:total], terms[2], LANES)
        small = (one[2 * total :] + two[total:]) + three
        return (small + (one[total : 2 * total] + two[:total])) + one[:total]

    now = stack(coeffs, 3)

    def gather(slot):
        speed = speeds_of(now, [t[slot] for t in (high, mid, low)])
        for a in range(2):
            speeds[a, slot] = speed[:, a * cells : (a + 1) * cells]

    gather(place)
    gather(beside)
    gather(across_of)
    outer = (ROW + 1) * core
    arrived(far)
    take(far)
    gather(far)
    scale = jnp.concatenate(
        [
            jnp.broadcast_to(slabs[s + 1, depth : depth + 1, :], (total, cells))
            for s in range(ROW)
        ],
        axis=0,
    )
    early = lax.broadcasted_iota(jnp.int32, (1, cells), 1) < across
    down = lax.broadcasted_iota(jnp.int32, (cells, cells), 0)
    right = lax.broadcasted_iota(jnp.int32, (cells, cells), 1)
    same = (down < across) == (right < across)
    apart = down - right
    apart = jnp.where(apart < 0, apart + across, apart)
    stencil = jnp.where(apart == 1, 8.0, 0.0) - jnp.where(apart == 2, 1.0, 0.0)
    stencil += jnp.where(apart == across - 2, 1.0, 0.0) - jnp.where(apart == across - 1, 8.0, 0.0)
    stencil = jnp.where(same, stencil, 0.0).astype(jnp.bfloat16)

    def cross_slope(f):
        height = f.shape[0]
        sums = product(stack(f, 3), stencil, ROWS)
        return (sums[2 * height :] + sums[height : 2 * height]) + sums[:height]

    def along_slope(f):
        swapped = pltpu.roll(f, across, 1)
        width = f.shape[0] - 2 * total

        def three(g):
            return g[:width], g[total : total + width], g[2 * total :]

        before, here, after = three(swapped)
        step = jnp.where(early, here - before, after - here)
        before, _, after = three(f)
        return (before - after) + 8.0 * step

    damping = viscosity * (1.0 / 144.0)
    inner = ROW * total
    nothing = jnp.zeros((2 * total, cells), jnp.float32)

    def across_part(middle):
        cross = cross_slope(jnp.concatenate(middle, axis=0))
        cross = [cross[:inner], cross[inner:]]
        return cross, cross_slope(jnp.concatenate([scale * f for f in cross], axis=0))

    def change_of(u, parts_across):
        middle = [f[total : total + inner] for f in u]
        along = [along_slope(f) for f in u]
        cross, spread_cross = parts_across
        fields = []
        for a in range(2):
            carried = (scale * (1.0 / 12.0)) * (middle[0] * along[a] + middle[1] * cross[a])
            damped = along_slope(jnp.concatenate([nothing, scale * along[a], nothing], axis=0))
            field = []
            for s in range(ROW + 2):
                f = damped[s * total : (s + 1) * total]
                if 1 <= s <= ROW:
                    at = slice((s - 1) * total, s * total)
                    f = f + spread_cross[a * inner : (a + 1) * inner][at]
                    field.append(carried[at] - damping * f)
                else:
                    field.append(-damping * f)
            fields.append(field)
        parts = [f[s] for s in range(ROW + 2) for f in fields]
        both = stack(jnp.concatenate(parts, axis=1), 2)
        size = (ROW + 2) * depth
        sums = product(both, high[...].reshape(size, -1), ROWS)
        rest = product(both[:total], mid[...].reshape(size, -1), ROWS)
        return (rest + sums[total:]) + sums[:total]

    def inside(u):
        return [f[total : total + inner] for f in u]

    own_part = across_part(
        [speeds[a, 1 : ROW + 1].reshape(inner, cells) for a in range(2)]
    )
    arrived(outer)
    send(0, outer, outer, partner)
    take(outer)
    gather(outer)
    arrived(ROW + 1 - outer)
    take(ROW + 1 - outer)
    gather(ROW + 1 - outer)

    change = change_of([speeds[a].reshape((ROW + 2) * total, cells) for a in range(2)], own_part)
    partial[...] = change
    spread(1, lambda r: partial, lambda d: landed.at[d - 1])
    waiting(landed, send_sem.at[3], small_sem.at[1]).wait_recv()
    coeffs = coeffs + TIME_STEP * (forcing - (change + jnp.sum(landed[...], axis=0)))
    now_ref[...] = coeffs.reshape(rows, own, -1)
    push_ref[...] = forcing.reshape(rows, own, -1)
    terms = [t[...].reshape((ROW + 2) * depth, -1) for t in (high, mid, low)]
    speed = speeds_of(stack(coeffs, 3), terms)
    u = []
    for a in range(2):
        starts = [s * depth + a * cells for s in range(ROW + 2)]
        u.append(jnp.concatenate([speed[:, i : i + cells] for i in starts], axis=0))
    last[...] = change_of(u, across_part(inside(u))).reshape(rows, own, -1)
    spread(2, lambda r: last.at[r], lambda d: last_landed.at[d - 1])
    waiting(last_landed, send_sem.at[4], small_sem.at[2]).wait_recv()
    change = last[row] + jnp.sum(last_landed[...], axis=0)
    out_ref[...] = now_ref[row] + TIME_STEP * (push_ref[row] - change)

    waiting(slabs.at[pl.ds(0, 4)], send_sem.at[0], recv_sem.at[0]).wait_send()

    @pl.when(first | final)
    def _():
        waiting(slabs.at[pl.ds(0, 2)], send_sem.at[1], recv_sem.at[0]).wait_send()

    waiting(picks.at[pl.ds(0, rows - 1)], send_sem.at[2], small_sem.at[0]).wait_send()
    waiting(landed, send_sem.at[3], small_sem.at[1]).wait_send()
    waiting(last_landed, send_sem.at[4], small_sem.at[2]).wait_send()


def shards(modes, cell_weight, seeds, coeff_table, force_table, visc_table):
    components, mode_count, layers, across = modes.shape
    n = lax.axis_size("space")
    rows = n // ROW
    cells = layers * across
    depth = components * cells
    own = seeds.shape[0]
    total = own * rows
    params = coeff_table.shape[0]
    f32, bf16 = jnp.float32, jnp.bfloat16
    return pl.pallas_call(
        functools.partial(kernel, n, across),
        out_shape=pltpu.VMEM((own, mode_count), f32),
        in_specs=[pl.BlockSpec(memory_space=pl.ANY)] * 6,
        out_specs=pl.BlockSpec(memory_space=pltpu.VMEM),
        scratch_shapes=[
            pltpu.VMEM((ROW + 2, depth + TAIL, mode_count), f32),
            pltpu.VMEM((ROW + 2, depth, mode_count), bf16),
            pltpu.VMEM((ROW + 2, depth, mode_count), bf16),
            pltpu.VMEM((ROW + 2, depth, mode_count), bf16),
            pltpu.VMEM((components, ROW + 2, total, cells), f32),
            pltpu.VMEM((layers, across), f32),
            pltpu.SMEM((own,), jnp.int32),
            pltpu.VMEM((1, params), f32),
            pltpu.VMEM((params, mode_count), f32),
            pltpu.VMEM((params, mode_count), f32),
            pltpu.VMEM((rows, own, 128), jnp.int32),
            pltpu.VMEM((total, mode_count), f32),
            pltpu.VMEM((rows - 1, total, mode_count), f32),
            pltpu.VMEM((rows, own, mode_count), f32),
            pltpu.VMEM((rows, own, mode_count), f32),
            pltpu.VMEM((rows, own, mode_count), f32),
            pltpu.VMEM((rows - 1, own, mode_count), f32),
            pltpu.SemaphoreType.DMA((6,)),
            pltpu.SemaphoreType.DMA((5,)),
            pltpu.SemaphoreType.DMA((ROW + 2,)),
            pltpu.SemaphoreType.DMA((3,)),
            pltpu.SemaphoreType.REGULAR((4,)),
        ],
        compiler_params=pltpu.CompilerParams(collective_id=0, has_side_effects=True),
    )(
        modes.transpose(0, 2, 3, 1).reshape(depth, mode_count),
        cell_weight,
        seeds,
        visc_table.reshape(1, -1),
        coeff_table,
        force_table,
    )


def solution(mesh):
    placed = (
        P("groups", None, "space", None),
        P("space", "groups"),
        P(("groups", "space")),
        P(),
        P(),
        P(),
    )
    return jax.shard_map(
        shards, mesh=mesh, in_specs=placed, out_specs=P(("groups", "space"), None), check_vma=False
    )
```

```python
import functools

import jax
import jax.numpy as jnp
from jax import lax
from jax.experimental import pallas as pl
from jax.experimental.pallas import tpu as pltpu
from jax.sharding import PartitionSpec as P

TIME_STEP = 0.5

MESH = pl.DeviceIdType.MESH

ROWS = ((1,), (0,))
LANES = ((1,), (1,))

ROW = 4

TAIL = 8


def product(a, b, contract):
    return lax.dot_general(a, b, (contract, ((), ())), preferred_element_type=jnp.float32)


def split(x, count):
    terms = []
    for _ in range(count):
        terms.append(x.astype(jnp.bfloat16))
        x = x - terms[-1].astype(jnp.float32)
    return terms


def stack(x, count):
    terms = []
    for _ in range(count):
        terms.append(x.astype(jnp.bfloat16).astype(jnp.float32))
        x = x - terms[-1]
    return jnp.concatenate(terms, axis=0).astype(jnp.bfloat16)


def kernel(
    n,
    across,
    modes_hbm,
    weight_hbm,
    seeds_hbm,
    visc_hbm,
    coeff_hbm,
    force_hbm,
    out_ref,
    slabs,
    high,
    mid,
    low,
    speeds,
    weight_ref,
    seeds_ref,
    visc_ref,
    coeff_ref,
    force_ref,
    picks,
    partial,
    landed,
    now_ref,
    push_ref,
    last,
    last_landed,
    load_sem,
    send_sem,
    recv_sem,
    small_sem,
    ok,
):
    me = lax.axis_index("space")
    rows = n // ROW
    row, seat = me // ROW, lax.rem(me, ROW)
    base = me - seat
    side, core = seat // 2, lax.rem(seat, 2)
    own = seeds_hbm.shape[0]
    depth = modes_hbm.shape[0]
    cells = depth // 2
    layers = weight_hbm.shape[0]
    params = coeff_hbm.shape[0]
    total = own * rows
    partner = me + 1 - 2 * core
    mirror = me + 2 - 4 * side
    above = lax.rem(row + 1, rows) * ROW
    below = lax.rem(row + rows - 1, rows) * ROW
    first, final = seat == 0, seat == ROW - 1
    place = seat + 1

    loads = [
        pltpu.make_async_copy(source, target, load_sem.at[i])
        for i, (source, target) in enumerate(
            (
                (modes_hbm, slabs.at[place, pl.ds(0, depth)]),
                (weight_hbm, weight_ref),
                (seeds_hbm, seeds_ref),
                (coeff_hbm, coeff_ref),
                (force_hbm, force_ref),
                (visc_hbm, visc_ref),
            )
        )
    ]
    for load in loads:
        load.start()

    barrier = pltpu.get_barrier_semaphore()

    def tell(peer):
        pl.semaphore_signal(barrier, inc=1, device_id={"space": peer}, device_id_type=MESH)

    def in_column(d):
        return lax.rem(me + ROW * d, n)

    bottom, top = row == 0, row == rows - 1

    @pl.when(core == 0)
    def _():
        tell(partner)

    @pl.when(side == 0)
    def _():
        tell(mirror)

    @pl.when(first & bottom)
    def _():
        tell(below + ROW - 1)
        tell(below + 1)

    @pl.when((seat == 2) & bottom)
    def _():
        tell(below + ROW - 1)

    @pl.when((seat == 1) & jnp.logical_not(top))
    def _():
        tell(above)

    @pl.when(final & jnp.logical_not(top))
    def _():
        tell(above)
        tell(above + 2)

    @pl.loop(row + 1, rows)
    def _(r):
        tell(r * ROW + seat)

    def answer(at, peer):
        pl.semaphore_signal(ok.at[at], inc=1, device_id={"space": peer}, device_id_type=MESH)

    def send(kind, source, target, peer):
        pltpu.make_async_remote_copy(
            src_ref=slabs.at[source],
            dst_ref=slabs.at[target],
            send_sem=send_sem.at[kind],
            recv_sem=recv_sem.at[target],
            device_id={"space": peer},
            device_id_type=MESH,
        ).start()

    def waiting(ref, send_at, recv_at):
        return pltpu.make_async_remote_copy(
            src_ref=ref,
            dst_ref=ref,
            send_sem=send_at,
            recv_sem=recv_at,
            device_id={"space": partner},
            device_id_type=MESH,
        )

    def arrived(slot):
        waiting(slabs.at[slot], send_sem.at[0], recv_sem.at[slot]).wait_recv()

    def spread(phase, source, target):
        @pl.loop(1, rows)
        def _(d):
            pltpu.make_async_remote_copy(
                src_ref=source(lax.rem(row + d, rows)),
                dst_ref=target(d),
                send_sem=send_sem.at[2 + phase],
                recv_sem=small_sem.at[phase],
                device_id={"space": in_column(d)},
                device_id_type=MESH,
            ).start()

    loads[2].wait()
    row_of = lax.broadcasted_iota(jnp.int32, (own, 128), 0)
    picked = jnp.zeros((own, 128), jnp.int32)
    for r in range(own):
        picked = jnp.where(row_of == r, seeds_ref[r], picked)
    picks[row] = picked
    loads[1].wait()
    weight = [weight_ref[s : s + 1, :] for s in range(layers)]
    slabs[place, depth : depth + 1, :] = jnp.concatenate(weight, axis=1) / (cells * n)
    loads[0].wait()

    def seeds_to(r):
        pltpu.make_async_remote_copy(
            src_ref=picks.at[row],
            dst_ref=picks.at[row],
            send_sem=send_sem.at[2],
            recv_sem=small_sem.at[0],
            device_id={"space": r * ROW + seat},
            device_id_type=MESH,
        ).start()

    def outer_down():
        send(1, place, ROW + 1, below + 1)
        send(1, place, ROW + 1, below + ROW - 1)

    def outer_up():
        send(1, place, 0, above)
        send(1, place, 0, above + 2)

    lower = core + side + row
    lower += jnp.where(jnp.logical_not(bottom) & first, 2, 0)
    lower += jnp.where(jnp.logical_not(bottom) & (seat == 2), 1, 0)
    lower += jnp.where(top & final, 2, 0) + jnp.where(top & (seat == 1), 1, 0)
    @pl.when(lower > 0)
    def _():
        pl.semaphore_wait(barrier, lower)

    @pl.when(core == 1)
    def _():
        answer(0, partner)
        send(0, place, place, partner)

    @pl.when(side == 1)
    def _():
        answer(1, mirror)
        send(0, place, place, mirror)

    @pl.when(top & final)
    def _():
        answer(2, above)

    @pl.when(top & (seat == 1))
    def _():
        answer(2, above)

    @pl.when(jnp.logical_not(bottom) & (first | (seat == 2)))
    def _():
        answer(2, below + ROW - 1)

    @pl.loop(0, row)
    def _(r):
        answer(3, r * ROW + seat)
        seeds_to(r)

    @pl.when(first & jnp.logical_not(bottom))
    def _():
        outer_down()

    @pl.when(final & top)
    def _():
        outer_up()

    @pl.when(core == 0)
    def _():
        pl.semaphore_wait(ok.at[0], 1)
        send(0, place, place, partner)

    @pl.when(side == 0)
    def _():
        pl.semaphore_wait(ok.at[1], 1)
        send(0, place, place, mirror)

    @pl.when(final & jnp.logical_not(top))
    def _():
        pl.semaphore_wait(ok.at[2], 2)
        outer_up()

    @pl.when(first & bottom)
    def _():
        pl.semaphore_wait(ok.at[2], 2)
        outer_down()

    @pl.when(jnp.logical_not(top))
    def _():
        pl.semaphore_wait(ok.at[3], rows - 1 - row)

    @pl.loop(row + 1, rows)
    def _(r):
        seeds_to(r)

    def take(slot):
        high[slot], mid[slot], low[slot] = split(slabs[slot, 0:depth, :], 3)

    across_of = seat + 2 - 4 * side + 1
    beside = partner - base + 1
    far = mirror + 1 - 2 * core - base + 1
    take(place)
    arrived(beside)
    take(beside)
    arrived(across_of)
    send(0, across_of, across_of, partner)
    take(across_of)

    for load in loads[3:]:
        load.wait()
    waiting(picks.at[pl.ds(0, rows - 1)], send_sem.at[2], small_sem.at[0]).wait_recv()
    picked = jnp.concatenate([picks[...].reshape(total, 128)] * (params // 128), axis=1)
    chosen = picked == lax.broadcasted_iota(jnp.int32, (total, params), 1)
    viscosity = jnp.sum(jnp.where(chosen, visc_ref[...], 0.0), axis=1, keepdims=True)
    chosen = chosen.astype(jnp.float32)
    coeffs = lax.dot(chosen, coeff_ref[...], precision=lax.Precision.HIGHEST)
    forcing = lax.dot(chosen, force_ref[...], precision=lax.Precision.HIGHEST)

    def speeds_of(now, terms):
        one = product(now, terms[0], LANES)
        two = product(now[: 2 * total], terms[1], LANES)
        three = product(now[:total], terms[2], LANES)
        small = (one[2 * total :] + two[total:]) + three
        return (small + (one[total : 2 * total] + two[:total])) + one[:total]

    now = stack(coeffs, 3)

    def gather(slot):
        speed = speeds_of(now, [t[slot] for t in (high, mid, low)])
        for a in range(2):
            speeds[a, slot] = speed[:, a * cells : (a + 1) * cells]

    gather(place)
    gather(beside)
    gather(across_of)
    outer = (ROW + 1) * core
    arrived(far)
    take(far)
    gather(far)
    scale = jnp.concatenate(
        [
            jnp.broadcast_to(slabs[s + 1, depth : depth + 1, :], (total, cells))
            for s in range(ROW)
        ],
        axis=0,
    )
    early = lax.broadcasted_iota(jnp.int32, (1, cells), 1) < across
    down = lax.broadcasted_iota(jnp.int32, (cells, cells), 0)
    right = lax.broadcasted_iota(jnp.int32, (cells, cells), 1)
    same = (down < across) == (right < across)
    apart = down - right
    apart = jnp.where(apart < 0, apart + across, apart)
    stencil = jnp.where(apart == 1, 8.0, 0.0) - jnp.where(apart == 2, 1.0, 0.0)
    stencil += jnp.where(apart == across - 2, 1.0, 0.0) - jnp.where(apart == across - 1, 8.0, 0.0)
    stencil = jnp.where(same, stencil, 0.0).astype(jnp.bfloat16)

    def cross_slope(f, count):
        height = f.shape[0]
        sums = product(stack(f, count), stencil, ROWS)
        slope = sums[(count - 1) * height :]
        for k in reversed(range(count - 1)):
            slope = slope + sums[k * height : (k + 1) * height]
        return slope

    def along_slope(f):
        swapped = pltpu.roll(f, across, 1)
        width = f.shape[0] - 2 * total

        def three(g):
            return g[:width], g[total : total + width], g[2 * total :]

        before, here, after = three(swapped)
        step = jnp.where(early, here - before, after - here)
        before, _, after = three(f)
        return (before - after) + 8.0 * step

    damping = viscosity * (1.0 / 144.0)
    inner = ROW * total
    nothing = jnp.zeros((2 * total, cells), jnp.float32)

    def across_part(middle):
        cross = cross_slope(jnp.concatenate(middle, axis=0), 3)
        cross = [cross[:inner], cross[inner:]]
        return cross, cross_slope(jnp.concatenate([scale * f for f in cross], axis=0), 2)

    def change_of(u, parts_across):
        middle = [f[total : total + inner] for f in u]
        along = [along_slope(f) for f in u]
        cross, spread_cross = parts_across
        fields = []
        for a in range(2):
            carried = (scale * (1.0 / 12.0)) * (middle[0] * along[a] + middle[1] * cross[a])
            damped = along_slope(jnp.concatenate([nothing, scale * along[a], nothing], axis=0))
            field = []
            for s in range(ROW + 2):
                f = damped[s * total : (s + 1) * total]
                if 1 <= s <= ROW:
                    at = slice((s - 1) * total, s * total)
                    f = f + spread_cross[a * inner : (a + 1) * inner][at]
                    field.append(carried[at] - damping * f)
                else:
                    field.append(-damping * f)
            fields.append(field)
        parts = [f[s] for s in range(ROW + 2) for f in fields]
        both = stack(jnp.concatenate(parts, axis=1), 2)
        size = (ROW + 2) * depth
        sums = product(both, high[...].reshape(size, -1), ROWS)
        rest = product(both[:total], mid[...].reshape(size, -1), ROWS)
        return (rest + sums[total:]) + sums[:total]

    def inside(u):
        return [f[total : total + inner] for f in u]

    own_part = across_part(
        [speeds[a, 1 : ROW + 1].reshape(inner, cells) for a in range(2)]
    )
    arrived(outer)
    send(0, outer, outer, partner)
    take(outer)
    gather(outer)
    arrived(ROW + 1 - outer)
    take(ROW + 1 - outer)
    gather(ROW + 1 - outer)

    change = change_of([speeds[a].reshape((ROW + 2) * total, cells) for a in range(2)], own_part)
    partial[...] = change
    spread(1, lambda r: partial, lambda d: landed.at[d - 1])
    waiting(landed, send_sem.at[3], small_sem.at[1]).wait_recv()
    coeffs = coeffs + TIME_STEP * (forcing - (change + jnp.sum(landed[...], axis=0)))
    now_ref[...] = coeffs.reshape(rows, own, -1)
    push_ref[...] = forcing.reshape(rows, own, -1)
    terms = [t[...].reshape((ROW + 2) * depth, -1) for t in (high, mid, low)]
    speed = speeds_of(stack(coeffs, 3), terms)
    u = []
    for a in range(2):
        starts = [s * depth + a * cells for s in range(ROW + 2)]
        u.append(jnp.concatenate([speed[:, i : i + cells] for i in starts], axis=0))
    last[...] = change_of(u, across_part(inside(u))).reshape(rows, own, -1)
    spread(2, lambda r: last.at[r], lambda d: last_landed.at[d - 1])
    waiting(last_landed, send_sem.at[4], small_sem.at[2]).wait_recv()
    change = last[row] + jnp.sum(last_landed[...], axis=0)
    out_ref[...] = now_ref[row] + TIME_STEP * (push_ref[row] - change)

    waiting(slabs.at[pl.ds(0, 4)], send_sem.at[0], recv_sem.at[0]).wait_send()

    @pl.when(first | final)
    def _():
        waiting(slabs.at[pl.ds(0, 2)], send_sem.at[1], recv_sem.at[0]).wait_send()

    waiting(picks.at[pl.ds(0, rows - 1)], send_sem.at[2], small_sem.at[0]).wait_send()
    waiting(landed, send_sem.at[3], small_sem.at[1]).wait_send()
    waiting(last_landed, send_sem.at[4], small_sem.at[2]).wait_send()


def shards(modes, cell_weight, seeds, coeff_table, force_table, visc_table):
    components, mode_count, layers, across = modes.shape
    n = lax.axis_size("space")
    rows = n // ROW
    cells = layers * across
    depth = components * cells
    own = seeds.shape[0]
    total = own * rows
    params = coeff_table.shape[0]
    f32, bf16 = jnp.float32, jnp.bfloat16
    return pl.pallas_call(
        functools.partial(kernel, n, across),
        out_shape=pltpu.VMEM((own, mode_count), f32),
        in_specs=[pl.BlockSpec(memory_space=pl.ANY)] * 6,
        out_specs=pl.BlockSpec(memory_space=pltpu.VMEM),
        scratch_shapes=[
            pltpu.VMEM((ROW + 2, depth + TAIL, mode_count), f32),
            pltpu.VMEM((ROW + 2, depth, mode_count), bf16),
            pltpu.VMEM((ROW + 2, depth, mode_count), bf16),
            pltpu.VMEM((ROW + 2, depth, mode_count), bf16),
            pltpu.VMEM((components, ROW + 2, total, cells), f32),
            pltpu.VMEM((layers, across), f32),
            pltpu.SMEM((own,), jnp.int32),
            pltpu.VMEM((1, params), f32),
            pltpu.VMEM((params, mode_count), f32),
            pltpu.VMEM((params, mode_count), f32),
            pltpu.VMEM((rows, own, 128), jnp.int32),
            pltpu.VMEM((total, mode_count), f32),
            pltpu.VMEM((rows - 1, total, mode_count), f32),
            pltpu.VMEM((rows, own, mode_count), f32),
            pltpu.VMEM((rows, own, mode_count), f32),
            pltpu.VMEM((rows, own, mode_count), f32),
            pltpu.VMEM((rows - 1, own, mode_count), f32),
            pltpu.SemaphoreType.DMA((6,)),
            pltpu.SemaphoreType.DMA((5,)),
            pltpu.SemaphoreType.DMA((ROW + 2,)),
            pltpu.SemaphoreType.DMA((3,)),
            pltpu.SemaphoreType.REGULAR((4,)),
        ],
        compiler_params=pltpu.CompilerParams(collective_id=0, has_side_effects=True),
    )(
        modes.transpose(0, 2, 3, 1).reshape(depth, mode_count),
        cell_weight,
        seeds,
        visc_table.reshape(1, -1),
        coeff_table,
        force_table,
    )


def solution(mesh):
    placed = (
        P("groups", None, "space", None),
        P("space", "groups"),
        P(("groups", "space")),
        P(),
        P(),
        P(),
    )
    return jax.shard_map(
        shards, mesh=mesh, in_specs=placed, out_specs=P(("groups", "space"), None), check_vma=False
    )
```
